256 devices in a mesh: freq: 64 (over x, z, y_lo), panel: 4 (over y_hi, core).
Axes of the slice: x: 4, y: 4 (y_hi: 2, y_lo: 2; y = y_hi * 2 + y_lo), z: 8, core: 2. Of those that a mesh axis runs over, the one named last changes fastest.
Arguments:
- reflection: bfloat16 [2, 64, 1024, 1024], P(None, 'freq', None, 'panel'), may hold values from -0.1875 to 0.1875
- tile_mask: int32 [64, 16, 16], P('freq', None, 'panel'), may hold values 0 or 1
- focusing: bfloat16 [2, 64, 1024, 256], P(None, 'freq', 'panel'), may hold values from -6 to 6
- initial: float32 [2, 64, 1024, 256], P(None, 'freq', 'panel'), may hold values from -6 to 6
- onsets: int32 [1024, 256], P(('freq', 'panel')), may hold values from 1 to 64
Outputs:
- updated: float32 [2, 64, 1024, 256], P(None, 'freq', 'panel')
The draws below stay inside these ranges and needn't reach their ends.
All inputs are finite; a program needn't handle non-finite values. No bound on the sum of `tile_mask` on one device may be relied on, other than what follows from the above.
Results may differ from the reference program's by a relative error of at most 0.0015.
Values may be sent and summed in bfloat16 or wider, within the bound.
No kernel may reach another device: no remote copies, remote signals or barrier semaphores. Data moves between devices by JAX's collectives and lax.ppermute only.
A program may use at most 64 MiB of HBM per device.

```python
import jax
import jax.numpy as jnp
from jax import lax

NF = 64
N = 1024
NV = 256
TILE = 64


def place_ends(array, own_key, low, high):
    index_at = [jax.random.randint(jax.random.fold_in(own_key, axis), (), 0, length) for axis, length in enumerate(array.shape)]
    main_axis = array.shape.index(max(array.shape))
    neighbour = index_at[:main_axis] + [(index_at[main_axis] + 1) % array.shape[main_axis]] + index_at[main_axis + 1:]
    return array.at[tuple(index_at)].set(low).at[tuple(neighbour)].set(high)


def block_scale(rng, shape, cuts, least, top_value):
    loudness, own = 1.0, jax.random.fold_in(rng, 6)
    for position, shards_of in cuts:
        steps = jnp.exp(jax.random.uniform(jax.random.fold_in(own, position), (shards_of,), jnp.float32, least / len(cuts), top_value / len(cuts)))
        loudness = loudness * jnp.repeat(steps, shape[position] // shards_of).reshape([-1 if axis == position else 1 for axis in range(len(shape))])
    return loudness


def bell_draw(rng, shape, width, bound, cuts=(), held_as=jnp.bfloat16):
    array = jax.random.normal(rng, shape, jnp.float32) * width
    if len(cuts) > 0:
        array = block_scale(rng, shape, cuts, -0.22, 0.18) * array
    return jnp.clip(array, min=-bound, max=bound).astype(held_as)


def setup_inputs(seed: int = 0) -> dict:
    key_list = jax.random.split(jax.random.key(seed), 6)
    return {
        "reflection": bell_draw(key_list[0], (2, NF, N, N), N ** -0.5, 0.1875, ((1, 64), (3, 4))),
        "tile_mask": place_ends((jax.random.randint(key_list[1], (NF, N // TILE, N // TILE), 0, 2) < 1).astype(jnp.int32), jax.random.fold_in(key_list[1], 1), 0, 1),
        "focusing": bell_draw(key_list[2], (2, NF, N, NV), 1.0, 6.0, ((1, 64), (2, 4))),
        "initial": bell_draw(key_list[3], (2, NF, N, NV), 1.0, 6.0, ((1, 64), (2, 4)), jnp.float32),
        "onsets": place_ends(jax.random.randint(key_list[4], (N, NV), 1, NF + 1), jax.random.fold_in(key_list[4], 1), 1, NF).astype(jnp.int32),
    }


def expand(occupied):
    filled = jnp.repeat(jnp.repeat(occupied, TILE, axis=0), TILE, axis=1)
    return filled.astype(jnp.bfloat16)


def matmul(left_arg, right_factor):
    return jnp.dot(left_arg, right_factor, preferred_element_type=jnp.float32)


def forward(operands):
    real_r, imag_r, occupied, real_f, imag_f = operands
    filled = expand(occupied)
    real_m = real_r * filled
    imag_m = imag_r * filled
    return (matmul(real_m, real_f) - matmul(imag_m, imag_f),
            matmul(real_m, imag_f) + matmul(imag_m, real_f))


def adjoint(operands):
    real_r, imag_r, occupied, real_w, imag_w = operands
    filled = expand(occupied)
    real_m = (real_r * filled).T
    imag_m = (imag_r * filled).T
    return (matmul(real_m, real_w) + matmul(imag_m, imag_w),
            matmul(real_m, imag_w) - matmul(imag_m, real_w))


def reference(reflection, tile_mask, focusing, initial, onsets):
    real_g, imag_g = lax.map(forward, (reflection[0], reflection[1], tile_mask, focusing[0], focusing[1]))
    series = jnp.fft.ifft(real_g + 1j * imag_g, axis=0)
    window = lax.iota(jnp.int32, NF)[:, None, None] < onsets[None]
    series = jnp.where(window, series, 0)
    spectrum = jnp.fft.fft(series, axis=0)
    real_w = jnp.real(spectrum).astype(jnp.bfloat16)
    imag_w = jnp.imag(spectrum).astype(jnp.bfloat16)
    real_a, imag_a = lax.map(adjoint, (reflection[0], reflection[1], tile_mask, real_w, imag_w))
    return initial + jnp.stack([real_a, imag_a])
```

```python
import math

import jax
import jax.numpy as jnp
import numpy as np
from jax import lax
from jax.sharding import PartitionSpec as P

SCALE = 16.0
CORE = ((0, 1), (1, 0), (2, 3), (3, 2))
CHIP = ((0, 2), (1, 3), (2, 0), (3, 1))


def transform(length, rows, sign):
    counter = np.arange(length)
    angles = (counter[:, None] * counter[None, :] % length) * (2.0 * math.pi / length)
    cosine, sine = np.cos(angles), sign * np.sin(angles)
    small = np.stack([np.stack([cosine, -sine], -1), np.stack([sine, cosine], -1)], 1)
    full = np.einsum("acbd,jk->acjbdk", small, np.eye(rows))
    return full.reshape(2 * length * rows, 2 * length * rows).astype(np.float32)


def exact_dot(left, right):
    return jnp.dot(left, right, precision=lax.Precision.HIGHEST, preferred_element_type=jnp.float32)


def local(reflection, tile_mask, focusing, initial, onsets):
    sources, columns = reflection.shape[2], reflection.shape[3]
    points = focusing.shape[3]
    edge = sources // tile_mask.shape[1]
    groups = lax.axis_size("freq")
    panels = lax.axis_size("panel")
    rows = sources // groups // panels
    panel = lax.axis_index("panel")

    filled = jnp.broadcast_to(
        tile_mask[0].astype(jnp.bfloat16)[:, None, :, None],
        (tile_mask.shape[1], edge, tile_mask.shape[2], edge),
    ).reshape(sources, columns)
    masked = reflection[:, 0] * filled
    masked = masked.reshape(2, groups, 2, 2, rows, columns)
    masked = jnp.where(panel // 2 == 0, masked, masked[:, :, ::-1])
    masked = jnp.where(panel % 2 == 0, masked, masked[:, :, :, ::-1])
    masked = masked.transpose(2, 3, 1, 0, 4, 5)
    turned = jnp.stack([-masked[:, :, :, 1], masked[:, :, :, 0]], 3)
    block = groups * 2 * rows
    operator = jnp.concatenate([masked, turned], -1).reshape(2, 2, block, 2 * columns)

    fields = focusing.reshape(2 * columns, points)
    partial = jnp.einsum("hcsr,rv->hcsv", operator, fields, preferred_element_type=jnp.float32)
    partial = partial * SCALE
    other = lax.ppermute(partial[:, 1].astype(jnp.float16), "panel", CORE)
    partial = partial[:, 0] + other.astype(jnp.float32)
    other = lax.ppermute(partial[1].astype(jnp.float16), "panel", CHIP)
    partial = partial[0] + other.astype(jnp.float32)

    traces = lax.all_to_all(
        partial.astype(jnp.float16).reshape(groups, 2 * rows, points), "freq",
        split_axis=0, concat_axis=0, tiled=True,
    ).reshape(block, points)
    to_time = jnp.asarray(transform(groups, rows, 1) / (SCALE * groups))
    to_freq = jnp.asarray(transform(groups, rows, -1))
    series = exact_dot(to_time, traces.astype(jnp.float32)).reshape(groups, 2, rows, points)
    inside = lax.broadcasted_iota(jnp.int32, series.shape, 0) < onsets
    series = jnp.where(inside, series, 0.0).reshape(block, points)
    windowed = exact_dot(to_freq, series).astype(jnp.bfloat16)

    own = lax.all_to_all(
        windowed.reshape(groups, 2 * rows, points), "freq", split_axis=0, concat_axis=0, tiled=True
    ).reshape(block, points)
    pair = jnp.stack([own, lax.ppermute(own, "panel", CHIP)])
    every = jnp.stack([pair, lax.ppermute(pair, "panel", CORE)], 1)
    adjoint = jnp.einsum("hcsr,hcsv->rv", operator, every, preferred_element_type=jnp.float32)
    return initial + adjoint.reshape(initial.shape)


def solution(mesh):
    return jax.shard_map(
        local,
        mesh=mesh,
        in_specs=(
            P(None, "freq", None, "panel"),
            P("freq", None, "panel"),
            P(None, "freq", "panel", None),
            P(None, "freq", "panel", None),
            P(("freq", "panel"), None),
        ),
        out_specs=P(None, "freq", "panel", None),
        check_vma=False,
    )
```

```python
import math

import jax
import jax.numpy as jnp
import numpy as np
from jax import lax
from jax.experimental import pallas as pl
from jax.experimental.pallas import tpu as pltpu
from jax.sharding import PartitionSpec as P

SCALE = 16.0
VMEM = 24 << 20
CORE = ((0, 1), (1, 0), (2, 3), (3, 2))
CHIP = ((0, 2), (1, 3), (2, 0), (3, 1))
F32, BF16, F16 = jnp.float32, jnp.bfloat16, jnp.float16


def transform(length, rows):
    counter = np.arange(length)
    angles = (counter[:, None] * counter[None, :] % length) * (2.0 * math.pi / length)
    cosine, sine = np.cos(angles), np.sin(angles)
    small = np.stack([np.stack([cosine, -sine], -1), np.stack([sine, cosine], -1)], 1)
    full = np.einsum("acbd,jk->acjbdk", small, np.eye(rows))
    full = full.reshape(2 * length * rows, 2 * length * rows).astype(np.float32)
    high = full.astype(BF16)
    return high, (full - high.astype(np.float32)).astype(BF16)


def dot(left, right):
    return jnp.dot(left, right, preferred_element_type=F32)


def masked_rows(operator_ref, mask_ref):
    _, groups, _, eight, columns = operator_ref.shape
    tiles, bands = mask_ref.shape
    lane = lax.broadcasted_iota(jnp.int32, (1, columns), 1) // (columns // tiles)
    keep = []
    for band in range(bands):
        row = jnp.zeros((1, columns), F32)
        for tile in range(tiles):
            row = jnp.where(lane == tile, mask_ref[tile, band].astype(F32), row)
        keep.append(jnp.broadcast_to(row, (groups * eight // bands, columns)).astype(BF16))
    keep = jnp.concatenate(keep, 0)
    return [operator_ref[part, :, 0].reshape(groups * eight, columns) * keep for part in (0, 1)]


def forward_kernel(where_ref, operator_ref, mask_ref, field_ref, out_ref):
    groups, eight, points = out_ref.shape[1:]
    real, imag = masked_rows(operator_ref, mask_ref)
    field_re, field_im = field_ref[0] * SCALE, field_ref[1] * SCALE
    fields = jnp.concatenate(
        [jnp.concatenate([field_re, field_im], 1), jnp.concatenate([-field_im, field_re], 1)], 0
    )
    sums = dot(jnp.concatenate([real, imag], 1), fields)
    real = sums[:, :points].reshape(groups, eight, points)
    imag = sums[:, points:].reshape(groups, eight, points)
    first = lax.broadcasted_iota(jnp.int32, real.shape, 1) < eight // 2
    core = where_ref[1]
    out_ref[core] = jnp.where(first, real, pltpu.roll(imag, eight // 2, axis=1))
    out_ref[1 - core] = jnp.where(first, pltpu.roll(real, eight // 2, axis=1), imag)


def adjoint_kernel(where_ref, operator_ref, mask_ref, own_ref, other_ref, base_ref, out_ref):
    groups, eight, points = own_ref.shape
    columns = operator_ref.shape[-1]
    real, imag = masked_rows(operator_ref, mask_ref)
    own, other = own_ref[...].astype(F32), other_ref[...].astype(F32)
    is_first = where_ref[1] == 0
    low, high = jnp.where(is_first, own, other), jnp.where(is_first, other, own)
    first = lax.broadcasted_iota(jnp.int32, low.shape, 1) < eight // 2
    field_re = jnp.where(first, low, pltpu.roll(high, eight // 2, axis=1))
    field_im = jnp.where(first, pltpu.roll(low, eight // 2, axis=1), high)
    field_re = field_re.reshape(groups * eight, points).astype(BF16)
    field_im = field_im.reshape(groups * eight, points).astype(BF16)
    fields = jnp.concatenate(
        [jnp.concatenate([field_re, field_im], 1), jnp.concatenate([field_im, -field_re], 1)], 0
    )
    sums = lax.dot_general(
        jnp.concatenate([real, imag], 0), fields, (((0,), (0,)), ((), ())), preferred_element_type=F32
    )
    out_ref[:columns] = base_ref[:columns] + sums[:, :points]
    out_ref[columns:] = base_ref[columns:] + sums[:, points:]


def split_dot(high_ref, low_ref, field):
    top = field.astype(BF16)
    rest = (field - top.astype(F32)).astype(BF16)
    high = high_ref[...]
    return dot(high, top) + (dot(low_ref[...], top) + dot(high, rest))


def window_kernel(high_ref, low_ref, traces_ref, onsets_ref, out_ref):
    length, eight, points = out_ref.shape
    shape = (length, eight, points)
    rows = length * eight
    series = split_dot(high_ref, low_ref, traces_ref[...]).reshape(shape)
    onsets = jnp.concatenate([onsets_ref[...]] * 2, 0)
    inside = lax.broadcasted_iota(jnp.int32, shape, 0) < onsets[None]
    sign = jnp.where(lax.broadcasted_iota(jnp.int32, shape, 1) < eight // 2, 1.0, -1.0)
    series = jnp.where(inside, series * (sign * (1.0 / (SCALE * length))), 0.0)
    windowed = split_dot(high_ref, low_ref, series.reshape(rows, points)).reshape(shape)
    out_ref[...] = (windowed * sign).reshape(rows, points).astype(BF16).reshape(shape)


def chosen_rows(operator, half):
    parts, groups, _, eight, columns = operator.shape
    return pl.BlockSpec(
        (parts, groups, 1, eight, columns),
        lambda step, where: (0, 0, where[0] if half == 0 else 1 - where[0], 0, 0),
    )


def whole(array):
    return pl.BlockSpec(array.shape, lambda step, where: (0,) * array.ndim)


SCALARS = pl.BlockSpec(memory_space=pltpu.SMEM)


def call(kernel, name, half, where, operator, mask, others, shape, flops):
    size = math.prod(shape) * 4 + operator.size + sum(o.size * o.dtype.itemsize for o in others)
    return pl.pallas_call(
        kernel,
        name=name,
        grid_spec=pltpu.PrefetchScalarGridSpec(
            num_scalar_prefetch=1,
            grid=(1,),
            in_specs=[chosen_rows(operator, half), SCALARS] + [whole(o) for o in others],
            out_specs=pl.BlockSpec(shape, lambda step, where: (0,) * len(shape)),
        ),
        out_shape=jax.ShapeDtypeStruct(shape, F32),
        cost_estimate=pl.CostEstimate(flops=flops, bytes_accessed=size, transcendentals=0),
        compiler_params=pltpu.CompilerParams(vmem_limit_bytes=VMEM),
    )(where, operator, mask, *others)


def local(reflection, tile_mask, focusing, initial, onsets):
    sources, columns = reflection.shape[2], reflection.shape[3]
    points = focusing.shape[3]
    groups = lax.axis_size("freq")
    rows = sources // groups // lax.axis_size("panel")
    eight = 2 * rows
    panel = lax.axis_index("panel")
    where = jnp.stack([panel >> 1, panel & 1])
    operator = reflection.reshape(2, groups, 2, eight, columns)
    mask = tile_mask[0].T
    fields = focusing[:, 0]
    work = 4 * sources * columns * points

    def forward(half):
        return call(
            forward_kernel, "forward", half, where, operator, mask, [fields],
            (2, groups, eight, points), work,
        )

    def reduce_core(partial):
        return partial[0] + lax.ppermute(partial[1].astype(F16), "panel", CORE).astype(F32)

    away = reduce_core(forward(1))
    arrived = lax.ppermute(away.astype(F16), "panel", CHIP)
    total = reduce_core(forward(0)) + arrived.astype(F32)
    traces = lax.all_to_all(total.astype(F16), "freq", split_axis=0, concat_axis=0, tiled=True)

    high, low = (jnp.asarray(m) for m in transform(groups, rows))
    flat = traces.astype(F32).reshape(groups * eight, points)
    windowed = pl.pallas_call(
        window_kernel,
        name="window",
        out_shape=jax.ShapeDtypeStruct((groups, eight, points), BF16),
        compiler_params=pltpu.CompilerParams(vmem_limit_bytes=VMEM),
    )(high, low, flat, onsets)

    own = lax.all_to_all(windowed, "freq", split_axis=0, concat_axis=0, tiled=True)
    far = lax.ppermute(own, "panel", CHIP)
    own_pair = lax.ppermute(own, "panel", CORE)
    base = initial.reshape(2 * columns, points)

    def adjoint(half, near, partner, base):
        return call(
            adjoint_kernel, "adjoint", half, where, operator, mask, [near, partner, base],
            base.shape, work,
        )

    updated = adjoint(0, own, own_pair, base)
    updated = adjoint(1, far, lax.ppermute(far, "panel", CORE), updated)
    return updated.reshape(initial.shape)


def solution(mesh):
    return jax.shard_map(
        local,
        mesh=mesh,
        in_specs=(
            P(None, "freq", None, "panel"),
            P("freq", None, "panel"),
            P(None, "freq", "panel", None),
            P(None, "freq", "panel", None),
            P(("freq", "panel"), None),
        ),
        out_specs=P(None, "freq", "panel", None),
        check_vma=False,
    )
```

```python
import functools
import math

import jax
import jax.numpy as jnp
import numpy as np
from jax import lax
from jax.experimental import pallas as pl
from jax.experimental.pallas import tpu as pltpu
from jax.sharding import PartitionSpec as P

SCALE = 16.0
VMEM = 24 << 20
CORE = ((0, 1), (1, 0), (2, 3), (3, 2))
CHIP = ((0, 2), (1, 3), (2, 0), (3, 1))
F32, BF16, F16 = jnp.float32, jnp.bfloat16, jnp.float16


def transform(length, rows):
    counter = np.arange(length)
    angles = (counter[:, None] * counter[None, :] % length) * (2.0 * math.pi / length)
    cosine, sine = np.cos(angles), np.sin(angles)
    small = np.stack([np.stack([cosine, -sine], -1), np.stack([sine, cosine], -1)], 1)
    full = np.einsum("acbd,jk->acjbdk", small, np.eye(rows))
    full = full.reshape(2 * length * rows, 2 * length * rows).astype(np.float32)
    high = full.astype(BF16)
    return np.stack([high, (full - high.astype(np.float32)).astype(BF16)])


def dot(left, right):
    return jnp.dot(left, right, preferred_element_type=F32)


def position():
    panel = lax.axis_index("panel")
    return panel >> 1, panel & 1


def masked_rows(rows_ref, mask_ref):
    groups, eight, columns = rows_ref.shape[1:]
    tiles, bands = mask_ref.shape
    lane = lax.broadcasted_iota(jnp.int32, (1, columns), 1) // (columns // tiles)
    keep = []
    for band in range(bands):
        row = jnp.zeros((1, columns), F32)
        for tile in range(tiles):
            row = jnp.where(lane == tile, mask_ref[tile, band].astype(F32), row)
        keep.append(jnp.broadcast_to(row, (groups * eight // bands, columns)).astype(BF16))
    keep = jnp.concatenate(keep, 0)
    return [rows_ref[part].reshape(groups * eight, columns) * keep for part in (0, 1)]


def forward_kernel(
    away, operator_ref, mask_ref, field_ref, out_ref, rows_ref, fields_ref, tiles_ref, sems
):
    groups, eight, points = out_ref.shape[1:]
    chip, core = position()
    half = 1 - chip if away else chip
    copies = [
        pltpu.make_async_copy(mask_ref, tiles_ref, sems.at[0]),
        pltpu.make_async_copy(operator_ref.at[0, :, half], rows_ref.at[0], sems.at[1]),
        pltpu.make_async_copy(operator_ref.at[1, :, half], rows_ref.at[1], sems.at[2]),
        pltpu.make_async_copy(field_ref, fields_ref, sems.at[3]),
    ]
    for copy in copies:
        copy.start()
    for copy in copies:
        copy.wait()
    real, imag = masked_rows(rows_ref, tiles_ref)
    field_re, field_im = fields_ref[0] * SCALE, fields_ref[1] * SCALE
    fields = jnp.concatenate(
        [jnp.concatenate([field_re, field_im], 1), jnp.concatenate([-field_im, field_re], 1)], 0
    )
    sums = dot(jnp.concatenate([real, imag], 1), fields)
    real = sums[:, :points].reshape(groups, eight, points)
    imag = sums[:, points:].reshape(groups, eight, points)
    first = lax.broadcasted_iota(jnp.int32, real.shape, 1) < eight // 2
    out_ref[core] = jnp.where(first, real, pltpu.roll(imag, eight // 2, axis=1))
    out_ref[1 - core] = jnp.where(first, pltpu.roll(real, eight // 2, axis=1), imag)


def ordered_fields(own_ref, other_ref):
    groups, eight, points = own_ref.shape
    own, other = own_ref[...].astype(F32), other_ref[...].astype(F32)
    is_first = position()[1] == 0
    low, high = jnp.where(is_first, own, other), jnp.where(is_first, other, own)
    first = lax.broadcasted_iota(jnp.int32, low.shape, 1) < eight // 2
    field_re = jnp.where(first, low, pltpu.roll(high, eight // 2, axis=1))
    field_im = jnp.where(first, pltpu.roll(low, eight // 2, axis=1), high)
    field_re = field_re.reshape(groups * eight, points).astype(BF16)
    field_im = field_im.reshape(groups * eight, points).astype(BF16)
    return jnp.concatenate(
        [jnp.concatenate([field_re, field_im], 1), jnp.concatenate([field_im, -field_re], 1)], 0
    )


def near_kernel(
    operator_ref, mask_ref, own_ref, other_ref, initial_ref, out_ref, far_ref,
    rows_ref, base_ref, tiles_ref, sems,
):
    columns, points = operator_ref.shape[-1], own_ref.shape[-1]
    chip, _ = position()
    copies = [
        pltpu.make_async_copy(mask_ref, tiles_ref, sems.at[0]),
        pltpu.make_async_copy(operator_ref.at[:, :, chip], rows_ref.at[0], sems.at[1]),
        pltpu.make_async_copy(operator_ref.at[:, :, 1 - chip], rows_ref.at[1], sems.at[2]),
        pltpu.make_async_copy(initial_ref, base_ref, sems.at[3]),
    ]
    for copy in copies:
        copy.start()
    for copy in copies:
        copy.wait()
    near, far = (jnp.concatenate(masked_rows(rows_ref.at[k], tiles_ref), 0) for k in (0, 1))
    far_ref[...] = far.T
    sums = lax.dot_general(
        near, ordered_fields(own_ref, other_ref), (((0,), (0,)), ((), ())),
        preferred_element_type=F32,
    )
    out_ref[:columns] = base_ref[:columns] + sums[:, :points]
    out_ref[columns:] = base_ref[columns:] + sums[:, points:]


def add_far(far_ref, own_ref, other_ref, base_ref, out_ref, lanes):
    columns, points = far_ref.shape[0], own_ref.shape[-1]
    sums = dot(far_ref[...], ordered_fields(own_ref, other_ref))
    out_ref[:columns] = base_ref[:columns, lanes] + sums[:, :points]
    out_ref[columns:] = base_ref[columns:, lanes] + sums[:, points:]


def middle_kernel(far_ref, own_ref, other_ref, base_ref, out_ref):
    add_far(far_ref, own_ref, other_ref, base_ref, out_ref, slice(0, own_ref.shape[-1]))


def last_kernel(far_ref, own_ref, other_ref, base_ref, done_ref, out_ref, rest_ref, sems):
    points = own_ref.shape[-1]
    early = pltpu.make_async_copy(done_ref, out_ref.at[:, :points], sems.at[0])
    early.start()
    add_far(far_ref, own_ref, other_ref, base_ref, rest_ref, slice(points, 2 * points))
    late = pltpu.make_async_copy(rest_ref, out_ref.at[:, points:], sems.at[1])
    late.start()
    early.wait()
    late.wait()


def split_dot(pair_ref, field):
    top = field.astype(BF16)
    rest = (field - top.astype(F32)).astype(BF16)
    high = pair_ref[0]
    return dot(high, top) + (dot(pair_ref[1], top) + dot(high, rest))


def window_kernel(pair_ref, traces_ref, onsets_ref, out_ref):
    length, eight, points = out_ref.shape
    shape = (length, eight, points)
    rows = length * eight
    series = split_dot(pair_ref, traces_ref[...]).reshape(shape)
    onsets = jnp.concatenate([onsets_ref[...]] * 2, 0)
    inside = lax.broadcasted_iota(jnp.int32, shape, 0) < onsets[None]
    sign = jnp.where(lax.broadcasted_iota(jnp.int32, shape, 1) < eight // 2, 1.0, -1.0)
    series = jnp.where(inside, series * (sign * (1.0 / (SCALE * length))), 0.0)
    windowed = split_dot(pair_ref, series.reshape(rows, points)).reshape(shape)
    out_ref[...] = (windowed * sign).reshape(rows, points).astype(BF16).reshape(shape)


HERE = pl.BlockSpec(memory_space=pltpu.HBM)
NEAR = pl.BlockSpec(memory_space=pltpu.VMEM)


def call(kernel, name, ins, outs, scratch, args, flops):
    size = sum(math.prod(o.shape) * o.dtype.itemsize for o in [*args, *(s for _, s in outs)])
    args = [pltpu.with_memory_space_constraint(a, pltpu.HBM) if s is HERE else a for s, a in zip(ins, args)]
    made = pl.pallas_call(
        kernel,
        name=name,
        in_specs=ins,
        out_specs=[spec for spec, _ in outs],
        out_shape=[shape for _, shape in outs],
        scratch_shapes=scratch,
        cost_estimate=pl.CostEstimate(flops=flops, bytes_accessed=size, transcendentals=0),
        compiler_params=pltpu.CompilerParams(vmem_limit_bytes=VMEM),
    )(*args)
    return made if len(outs) > 1 else made[0]


def local(reflection, tile_mask, focusing, initial, onsets):
    sources, columns = reflection.shape[2], reflection.shape[3]
    points = focusing.shape[3]
    groups = lax.axis_size("freq")
    rows = sources // groups // lax.axis_size("panel")
    eight = 2 * rows
    operator = reflection.reshape(2, groups, 2, eight, columns)
    mask = tile_mask[0].T
    fields = focusing[:, 0]
    work = 4 * sources * columns * points
    shaped = jax.ShapeDtypeStruct
    tiles = pltpu.SMEM(mask.shape, jnp.int32)
    sems = pltpu.SemaphoreType.DMA((4,))
    rows_shape = (2, groups, eight, columns)

    def forward(away, fields):
        return call(
            functools.partial(forward_kernel, away), "forward", [HERE] * 3,
            [(NEAR, shaped((2, groups, eight, points), F32))],
            [pltpu.VMEM(rows_shape, BF16), pltpu.VMEM(fields.shape, BF16), tiles, sems],
            [operator, mask, fields], work,
        )

    def swap(array, pairs):
        return lax.ppermute(array, "panel", pairs)

    away = forward(True, fields)
    away = (away[0] + swap(away[1].astype(F16), CORE).astype(F32)).astype(F16)
    away, fields = lax.optimization_barrier((away, fields))
    total = forward(False, fields)
    arrived = swap(away, CHIP)
    total = total[0] + swap(total[1].astype(F16), CORE).astype(F32) + arrived.astype(F32)
    traces = lax.all_to_all(total.astype(F16), "freq", split_axis=0, concat_axis=0, tiled=True)

    pair = jnp.asarray(transform(groups, rows))
    flat = traces.astype(F32).reshape(groups * eight, points)
    windowed = call(
        window_kernel, "window", [NEAR] * 3, [(NEAR, shaped(traces.shape, BF16))], [],
        [pair, flat, onsets], 12 * flat.shape[0] ** 2 * points,
    )

    own = lax.all_to_all(windowed, "freq", split_axis=0, concat_axis=0, tiled=True)
    cut = points // 2
    far = [swap(own[:, :, :cut], CHIP), swap(own[:, :, cut:], CHIP)]
    base = shaped((2 * columns, points), F32)
    updated, turned = call(
        near_kernel, "near", [HERE] * 2 + [NEAR] * 2 + [HERE],
        [(NEAR, base), (NEAR, shaped((columns, sources), BF16))],
        [pltpu.VMEM((2, *rows_shape), BF16), pltpu.VMEM(base.shape, F32), tiles, sems],
        [operator, mask, own, swap(own, CORE), initial.reshape(base.shape)], work,
    )
    far[0], updated = lax.optimization_barrier((far[0], updated))
    done = call(
        middle_kernel, "middle", [NEAR] * 4, [(NEAR, shaped((2 * columns, cut), F32))], [],
        [turned, far[0], swap(far[0], CORE), updated], work // 2,
    )
    updated = call(
        last_kernel, "last", [NEAR] * 5, [(HERE, base)],
        [pltpu.VMEM((2 * columns, points - cut), F32), pltpu.SemaphoreType.DMA((2,))],
        [turned, far[1], swap(far[1], CORE), updated, done], work // 2,
    )
    return updated.reshape(initial.shape)


def solution(mesh):
    return jax.shard_map(
        local,
        mesh=mesh,
        in_specs=(
            P(None, "freq", None, "panel"),
            P("freq", None, "panel"),
            P(None, "freq", "panel", None),
            P(None, "freq", "panel", None),
            P(("freq", "panel"), None),
        ),
        out_specs=P(None, "freq", "panel", None),
        check_vma=False,
    )
```

```python
import functools
import math

import jax
import jax.numpy as jnp
import numpy as np
from jax import lax
from jax.experimental import pallas as pl
from jax.experimental.pallas import tpu as pltpu
from jax.sharding import Mesh, PartitionSpec as P

SCALE = 16.0
VMEM = 24 << 20
SWAP = ((0, 1), (1, 0))
CROSS = ((0, 3), (1, 2), (2, 1), (3, 0))
F32, BF16, F16 = jnp.float32, jnp.bfloat16, jnp.float16


def transform(length, rows):
    half = np.arange(length // 2)
    both = []
    for parity in (0, 1):
        turns = half[:, None] * (2 * half[None, :] + parity) % length
        angles = turns * (2.0 * math.pi / length)
        cosine, sine = np.cos(angles), np.sin(angles)
        small = np.stack([np.stack([cosine, -sine], -1), np.stack([sine, cosine], -1)], 1)
        full = np.einsum("acbd,jk->acjbdk", small, np.eye(rows))
        full = full.reshape(length * rows, length * rows).astype(np.float32)
        high = full.astype(BF16)
        both.append(np.stack([high, (full - high.astype(np.float32)).astype(BF16)]))
    return np.stack(both)


def dot(left, right):
    return jnp.dot(left, right, preferred_element_type=F32)


def position():
    return lax.axis_index("side"), lax.axis_index("chip"), lax.axis_index("core")


def recorded(mask_ref, columns):
    tiles, bands = mask_ref.shape
    lane = lax.broadcasted_iota(jnp.int32, (1, columns), 1) // (columns // tiles)
    keep = []
    for band in range(bands):
        row = jnp.zeros((1, columns), F32)
        for tile in range(tiles):
            row = jnp.where(lane == tile, mask_ref[tile, band].astype(F32), row)
        keep.append(row)
    return keep


def masked_rows(rows_ref, keep):
    groups, eight, columns = rows_ref.shape[1:]
    keep = jnp.concatenate(
        [jnp.broadcast_to(row, (groups * eight // len(keep), columns)).astype(BF16) for row in keep], 0
    )
    return [rows_ref[part].reshape(groups * eight, columns) * keep for part in (0, 1)]


def products(rows_ref, keep, fields, out_ref):
    _, chips, lines, eight, points = out_ref.shape
    _, chip, core = position()
    sums = dot(jnp.concatenate(masked_rows(rows_ref, keep), 1), fields)
    real = sums[:, :points].reshape(lines * chips, eight, points)
    imag = sums[:, points:].reshape(lines * chips, eight, points)
    first = lax.broadcasted_iota(jnp.int32, real.shape, 1) < eight // 2
    low = jnp.where(first, real, pltpu.roll(imag, eight // 2, axis=1))
    high = jnp.where(first, pltpu.roll(real, eight // 2, axis=1), imag)
    for target, value in ((core, low), (1 - core, high)):
        value = value.reshape(lines, chips, eight, points)
        out_ref[target, chip] = value[:, 0]
        out_ref[target, 1 - chip] = value[:, 1]


def other_kernel(
    operator_ref, mask_ref, field_ref, out_ref, rest_ref, fields_ref, keep_ref,
    rows_ref, field_vmem, tiles_ref, sems,
):
    side, _, _ = position()
    flat = rows_ref.shape
    copies = [
        pltpu.make_async_copy(mask_ref, tiles_ref, sems.at[0]),
        pltpu.make_async_copy(field_ref, field_vmem, sems.at[1]),
        pltpu.make_async_copy(operator_ref.at[:, :, 1 - side], rows_ref, sems.at[2]),
        pltpu.make_async_copy(operator_ref.at[:, :, side], rest_ref, sems.at[3]),
    ]
    for copy in copies:
        copy.start()
    copies[0].wait()
    keep = recorded(tiles_ref, flat[-1])
    for band, row in enumerate(keep):
        keep_ref[band : band + 1] = row
    copies[1].wait()
    field_re, field_im = field_vmem[0] * SCALE, field_vmem[1] * SCALE
    fields = jnp.concatenate(
        [jnp.concatenate([field_re, field_im], 1), jnp.concatenate([-field_im, field_re], 1)], 0
    )
    fields_ref[...] = fields
    copies[2].wait()
    groups = (flat[0], flat[1] * flat[2], *flat[3:])
    products(rows_ref.reshape(groups), keep, fields, out_ref)
    copies[3].wait()


def near_kernel(rows_ref, fields_ref, keep_ref, out_ref):
    flat = rows_ref.shape
    groups = (flat[0], flat[1] * flat[2], *flat[3:])
    keep = [keep_ref[band : band + 1] for band in range(keep_ref.shape[0])]
    products(rows_ref.reshape(groups), keep, fields_ref[...], out_ref)


def ordered_fields(own_ref, other_ref):
    groups, eight, points = own_ref.shape
    own, other = own_ref[...].astype(F32), other_ref[...].astype(F32)
    is_first = position()[2] == 0
    low, high = jnp.where(is_first, own, other), jnp.where(is_first, other, own)
    first = lax.broadcasted_iota(jnp.int32, low.shape, 1) < eight // 2
    field_re = jnp.where(first, low, pltpu.roll(high, eight // 2, axis=1))
    field_im = jnp.where(first, pltpu.roll(low, eight // 2, axis=1), high)
    field_re = field_re.reshape(groups * eight, points).astype(BF16)
    field_im = field_im.reshape(groups * eight, points).astype(BF16)
    return jnp.concatenate(
        [jnp.concatenate([field_re, field_im], 1), jnp.concatenate([field_im, -field_re], 1)], 0
    )


def turn_kernel(
    operator_ref, mask_ref, pairs_ref, out_ref, held_ref, rows_ref, tiles_ref, sems
):
    side, chip, _ = position()
    places = [(near, here) for near in (side, 1 - side) for here in (chip, 1 - chip)]
    copies = [
        pltpu.make_async_copy(mask_ref, tiles_ref, sems.at[4]),
        pltpu.make_async_copy(pairs_ref, held_ref, sems.at[5]),
    ] + [
        pltpu.make_async_copy(operator_ref.at[:, :, near, here], rows_ref.at[k], sems.at[k])
        for k, (near, here) in enumerate(places)
    ]
    for copy in copies:
        copy.start()
    for copy in copies:
        copy.wait()
    keep = recorded(tiles_ref, rows_ref.shape[-1])
    for k in range(len(places)):
        out_ref[k] = jnp.concatenate(masked_rows(rows_ref.at[k], keep), 0).T


def early_kernel(parts, turned_ref, base_ref, own_ref, other_ref, out_ref):
    columns, points = turned_ref.shape[1], base_ref.shape[1]
    sums = 0.0
    for place, part in enumerate(parts):
        fields = ordered_fields(own_ref.at[place], other_ref.at[place])
        sums = sums + dot(turned_ref[part], fields)
    out_ref[:columns] = base_ref[:columns] + sums[:, :points]
    out_ref[columns:] = base_ref[columns:] + sums[:, points:]


def last_kernel(part, turned_ref, base_ref, own_ref, other_ref, out_ref, held_ref, sems):
    columns, points = turned_ref.shape[1], base_ref.shape[1]
    fields = ordered_fields(own_ref, other_ref)
    half = columns // 2
    copies = []
    for k in range(4):
        lanes = slice(k // 2 * points, (k // 2 + 1) * points)
        sums = dot(turned_ref[part, k % 2 * half : (k % 2 + 1) * half], fields[:, lanes])
        span = pl.ds(k * half, half)
        held_ref[span] = base_ref[span] + sums
        copies.append(pltpu.make_async_copy(held_ref.at[span], out_ref.at[span], sems.at[k]))
        copies[-1].start()
    for copy in copies:
        copy.wait()


def split_dot(pair_ref, field, side):
    top = field.astype(BF16)
    rest = (field - top.astype(F32)).astype(BF16)

    def times(left, right):
        return lax.dot_general(left, right, (((side,), (0,)), ((), ())), preferred_element_type=F32)

    high = pair_ref[0]
    return times(high, top) + (times(pair_ref[1], top) + times(high, rest))


def window_kernel(pairs_ref, traces_ref, onsets_ref, out_ref, onset_ref, sem):
    lines, sides, eight, points = out_ref.shape
    shape = (lines, eight, points)
    rows = lines * eight
    side, _, _ = position()
    fetch = pltpu.make_async_copy(onsets_ref, onset_ref, sem)
    fetch.start()
    even = split_dot(pairs_ref.at[0], traces_ref[:, side].reshape(rows, points), 1)
    odd = split_dot(pairs_ref.at[1], traces_ref[:, 1 - side].reshape(rows, points), 1)
    fetch.wait()
    onsets = jnp.concatenate([onset_ref[...]] * 2, 0)[None]
    time = lax.broadcasted_iota(jnp.int32, shape, 0)
    scale = 1.0 / (SCALE * lines * sides)
    early = jnp.where(time < onsets, (even + odd).reshape(shape) * scale, 0.0)
    late = jnp.where(time + lines < onsets, (even - odd).reshape(shape) * scale, 0.0)
    even = split_dot(pairs_ref.at[0], (early + late).reshape(rows, points), 0)
    odd = split_dot(pairs_ref.at[1], (early - late).reshape(rows, points), 0)
    out_ref[:, side] = even.reshape(shape).astype(BF16)
    out_ref[:, 1 - side] = odd.reshape(shape).astype(BF16)


HERE = pl.BlockSpec(memory_space=pltpu.HBM)
NEAR = pl.BlockSpec(memory_space=pltpu.VMEM)


def call(kernel, ins, outs, scratch, args, flops):
    size = sum(math.prod(o.shape) * o.dtype.itemsize for o in [*args, *(s for _, s in outs)])
    args = [pltpu.with_memory_space_constraint(a, pltpu.HBM) if s is HERE else a for s, a in zip(ins, args)]
    run = pl.pallas_call(
        kernel,
        in_specs=ins,
        out_specs=[spec for spec, _ in outs],
        out_shape=[shape for _, shape in outs],
        scratch_shapes=scratch,
        cost_estimate=pl.CostEstimate(flops=flops, bytes_accessed=size, transcendentals=0),
        compiler_params=pltpu.CompilerParams(vmem_limit_bytes=VMEM),
    )
    made = run(*args)
    return made if len(outs) > 1 else made[0]


def step(reflection, tile_mask, focusing, initial, onsets):
    sources, columns = reflection.shape[2], reflection.shape[3]
    points = focusing.shape[3]
    lines, sides, chips = (lax.axis_size(name) for name in ("line", "side", "chip"))
    groups = lines * sides
    rows = sources // groups // chips // lax.axis_size("core")
    eight = 2 * rows
    operator = reflection[:, 0]
    mask = tile_mask[0].T
    fields = focusing[:, 0]
    work = 4 * sources * columns * points
    shaped = jax.ShapeDtypeStruct
    tiles = pltpu.SMEM(mask.shape, jnp.int32)

    def swap(array, *axes):
        return lax.ppermute(array, axes, SWAP if len(axes) == 1 else CROSS)

    def scatter(array):
        return lax.all_to_all(array, "line", split_axis=0, concat_axis=0, tiled=True)

    lined = operator.reshape(2, lines, sides, chips, eight, columns)
    piece = (2, lines, chips, eight, columns)
    made = shaped((2, chips, lines, eight, points), F32)
    other, rest, wide, keep = call(
        other_kernel, [HERE] * 3,
        [(NEAR, made), (NEAR, shaped(piece, BF16)),
         (NEAR, shaped((2 * columns, 2 * points), BF16)),
         (NEAR, shaped((mask.shape[1], columns), F32))],
        [pltpu.VMEM(piece, BF16), pltpu.VMEM(fields.shape, BF16), tiles,
         pltpu.SemaphoreType.DMA((4,))],
        [lined, mask, fields], work,
    )
    own = call(near_kernel, [NEAR] * 3, [(NEAR, made)], [], [rest, wide, keep], work)
    other = (other[0] + swap(other[1].astype(F16), "core").astype(F32)).astype(F16)
    own = own[0] + swap(own[1].astype(F16), "core").astype(F32)
    from_side, from_cross = swap(other[0], "side"), swap(other[1], "side", "chip")
    from_chip = swap(own[1].astype(F16), "chip")
    own, mask = lax.optimization_barrier((own, mask))
    pair = jnp.asarray(transform(groups, rows))
    turned, pair = call(
        turn_kernel, [HERE] * 3,
        [(NEAR, shaped((sides * chips, columns, 2 * lines * eight), BF16)),
         (NEAR, shaped(pair.shape, BF16))],
        [pltpu.VMEM((sides * chips, 2, lines, eight, columns), BF16), tiles,
         pltpu.SemaphoreType.DMA((6,))],
        [lined, mask, pair], work // 8,
    )
    from_chip, turned = lax.optimization_barrier((from_chip, turned))
    total = jnp.stack(
        [own[0] + from_chip.astype(F32), from_side.astype(F32) + from_cross.astype(F32)], 1
    )
    traces = scatter(total.astype(F16))

    windowed = call(
        window_kernel, [NEAR, NEAR, HERE], [(NEAR, shaped(traces.shape, BF16))],
        [pltpu.VMEM(onsets.shape, jnp.int32), pltpu.SemaphoreType.DMA],
        [pair, traces.astype(F32), onsets], 6 * (groups * eight) ** 2 * points,
    )

    mine = scatter(windowed)
    own, other = mine[:, 0], mine[:, 1]
    from_chip, from_side = swap(own, "chip"), swap(other, "side")
    from_cross = swap(other, "side", "chip")

    early = jnp.stack([own, from_side, from_cross])
    base = initial.reshape(2 * columns, points)
    updated = call(
        functools.partial(early_kernel, (0, 2, 3)), [NEAR] * 4,
        [(NEAR, shaped(base.shape, F32))], [],
        [turned, base, early, swap(early, "core")], work,
    )
    updated = call(
        functools.partial(last_kernel, 1), [NEAR] * 4, [(HERE, shaped(base.shape, F32))],
        [pltpu.VMEM(base.shape, F32), pltpu.SemaphoreType.DMA((4,))],
        [turned, updated, from_chip, swap(from_chip, "core")], work // 4,
    )
    return updated.reshape(initial.shape)


def solution(mesh):
    groups, panels = mesh.devices.shape
    split = Mesh(
        mesh.devices.reshape(groups // 2, 2, panels // 2, 2), ("line", "side", "chip", "core")
    )
    freq, panel = ("line", "side"), ("chip", "core")
    return jax.shard_map(
        step,
        mesh=split,
        in_specs=(
            P(None, freq, None, panel),
            P(freq, None, panel),
            P(None, freq, panel, None),
            P(None, freq, panel, None),
            P((*freq, *panel), None),
        ),
        out_specs=P(None, freq, panel, None),
        check_vma=False,
    )
```
